512 devices in a mesh: row: 16 (over y, x_hi, core), col: 32 (over x_lo, z).
Axes of the slice: x: 4 (x_hi: 2, x_lo: 2; x = x_hi * 2 + x_lo), y: 4, z: 16, core: 2. Of those that a mesh axis runs over, the one named last changes fastest.
Arguments:
- vectors: bfloat16 [393216, 1024], P(('row', 'col')), may hold values from -6 to 6
- ham_blocks: bfloat16 [3072, 5, 128, 128], P(('row', 'col')), as said below
- ham_columns: int32 [3072, 5], P(('row', 'col')), may hold values from 0 to 3071, as said below
- bounds: float32 [2], replicated, may hold values from -1 to 2.6, as said below
Outputs:
- filtered: bfloat16 [393216, 1024], P(('row', 'col'))
The draws below stay inside these ranges and needn't reach their ends.
Inputs may be any that keep to these rules, and one draw needn't show every extreme that they name: `ham_columns`: each slot of block row g names a block column (g + o) mod 3072 with -2 <= o <= 2; some slot names g itself, every other distance at most once. Slots whose offset is absent name g itself and carry zero blocks; the one slot with offset 0 carries the diagonal block. `ham_blocks`: H is symmetric: the block of block row g at block column h is the transpose of the block of block row h at block column g. bounds[0] < bounds[1].
All inputs are finite; a program needn't handle non-finite values.
Results may differ from the reference program's by a relative error of at most 0.0045.
Values may be sent and summed in bfloat16 or wider, within the bound.
A program may use at most 64 MiB of HBM per device.

```python
import math
import jax
import jax.numpy as jnp
from jax import lax

BLOCK = 128
VECTORS = 1024
REACH = 2
SLOTS = 5
DEG = 2
NBLOCKS = 3072
ORBITALS = 393216


def band_pattern(key):
    present_pair = jax.random.randint(jax.random.fold_in(key, 31), (NBLOCKS, REACH), 0, 5) < 3
    row_ids = jnp.arange(NBLOCKS, dtype=jnp.int32).reshape(-1, 1)
    distance = jnp.arange(1, REACH + 1, dtype=jnp.int32).reshape(1, -1)
    upward = present_pair
    downward = present_pair[jnp.remainder(row_ids - distance, NBLOCKS), distance - 1]
    present = jnp.concatenate([jnp.ones((NBLOCKS, 1), dtype=bool), upward, downward], axis=1)
    offsets = jnp.concatenate([jnp.zeros((1,), jnp.int32), jnp.arange(1, REACH + 1, dtype=jnp.int32), -jnp.arange(1, REACH + 1, dtype=jnp.int32)])
    order_keys = jax.random.split(jax.random.fold_in(key, 32), NBLOCKS)
    orders = jax.vmap(lambda item: jax.random.permutation(item, SLOTS))(order_keys).astype(jnp.int32)
    slot_offset = offsets[orders]
    slot_present = jnp.take_along_axis(present, orders, axis=1)
    columns = jnp.where(slot_present, jnp.remainder(row_ids + slot_offset, NBLOCKS), row_ids)
    return (columns.astype(jnp.int32), slot_offset, slot_present)


def draw_ham_columns(key, part):
    columns, slot_offset, slot_present = band_pattern(key)
    return columns


def draw_ham_blocks(key, part):
    columns, slot_offset, slot_present = band_pattern(key)
    row_ids = jnp.broadcast_to(jnp.arange(NBLOCKS, dtype=jnp.int32).reshape(-1, 1), columns.shape)
    value_key = jax.random.fold_in(key, 33)
    scale = float((1.0 + 1.2 * REACH) * BLOCK) ** (-0.5)

    def one_block(items):
        row_id = items[0]
        offset = items[1]
        alive = items[2]
        distance = jnp.abs(offset)
        lower = jnp.where(offset < 0, jnp.remainder(row_id + offset, NBLOCKS), row_id)
        item = jax.random.fold_in(value_key, lower * (REACH + 1) + distance)
        raw = jax.random.normal(item, (BLOCK, BLOCK), jnp.float32)
        flipped = jnp.swapaxes(raw, 0, 1)
        chosen = jnp.where(offset > 0, raw, jnp.where(offset < 0, flipped, (raw + flipped) * math.sqrt(0.5)))
        return (chosen * scale * alive.astype(jnp.float32)).astype(jnp.bfloat16)
    stacked = jnp.stack([row_ids.reshape(-1), slot_offset.reshape(-1), slot_present.reshape(-1).astype(jnp.int32)], axis=1)
    blocks = lax.map(one_block, stacked)
    return blocks.reshape(NBLOCKS, SLOTS, BLOCK, BLOCK)


def draw_bounds(key, part):
    low_key, high_key = jax.random.split(jax.random.fold_in(key, 21))
    lower = jax.random.uniform(low_key, (), jnp.float32, -1.0, -0.2)
    upper = jax.random.uniform(high_key, (), jnp.float32, 2.0, 2.6)
    return jnp.stack([lower, upper])


def level_of(own_key, extent, pieces, low, high):
    factor_of, own = 1.0, jax.random.fold_in(own_key, 6)
    for axis_at, shards_of in pieces:
        draws = jnp.exp(jax.random.uniform(jax.random.fold_in(own, axis_at), (shards_of,), jnp.float32, low / len(pieces), high / len(pieces)))
        factor_of = factor_of * jnp.repeat(draws, extent[axis_at] // shards_of).reshape([-1 if axis == axis_at else 1 for axis in range(len(extent))])
    return factor_of


def bell_draw(own_key, extent, width, most, cuts=(), held_as=jnp.bfloat16):
    gain = level_of(own_key, extent, cuts, -0.22, 0.18) if cuts else 1.0
    array = jax.random.normal(own_key, extent, jnp.float32) * width * gain
    return jnp.minimum(jnp.maximum(array, -most), most).astype(held_as)


def setup_inputs(seed: int = 0) -> dict:
    arg_keys = jax.random.split(jax.random.key(seed), 5)
    vectors = bell_draw(arg_keys[0], (ORBITALS, VECTORS), 1.0, 6.0, ((0, 512),))
    ham_blocks = draw_ham_blocks(jax.random.fold_in(arg_keys[4], 71), 0)
    ham_columns = draw_ham_columns(jax.random.fold_in(arg_keys[4], 71), 0)
    bounds = draw_bounds(jax.random.fold_in(arg_keys[4], 71), 0)
    return dict(vectors=vectors, ham_blocks=ham_blocks, ham_columns=ham_columns, bounds=bounds)


def apply_hamiltonian(current, ham_blocks, ham_columns):
    grid = current.reshape(NBLOCKS, BLOCK, VECTORS)

    def one_row(index):
        blocks = ham_blocks[index].astype(jnp.float32)
        picked = grid[ham_columns[index].astype(jnp.int32)].astype(jnp.float32)
        return jnp.einsum("kij,kjm->im", blocks, picked, precision=lax.Precision.HIGHEST)

    image = lax.map(one_row, jnp.arange(NBLOCKS, dtype=jnp.int32))
    return image.reshape(NBLOCKS * BLOCK, VECTORS)


def reference(vectors, ham_blocks, ham_columns, bounds):
    center = 0.5 * (bounds[1] + bounds[0])
    halfwidth = 0.5 * (bounds[1] - bounds[0])
    previous = vectors
    current = vectors
    for degree_step in range(DEG):
        image = apply_hamiltonian(current, ham_blocks, ham_columns)
        shifted = (image - center * current.astype(jnp.float32)) / halfwidth
        if degree_step == 0:
            updated = shifted
        else:
            updated = 2.0 * shifted - previous.astype(jnp.float32)
        previous, current = current, updated.astype(jnp.bfloat16)
    return current
```

```python
import functools

import jax
import jax.numpy as jnp
from jax import lax
from jax.experimental import pallas as pl
from jax.experimental.pallas import tpu as pltpu
from jax.sharding import PartitionSpec as P

REACH = 2
MESH = pl.DeviceIdType.MESH
F32 = jnp.float32
BF16 = jnp.bfloat16
CHUNKS = 4


def dot(a, b):
    return jnp.dot(a, b, preferred_element_type=F32)


def kernel(
    rows_n, cols_n, chunks,
    bounds_ref, columns_ref, vec_hbm, ham_hbm, out_hbm,
    ham, band, turned, vec, halo, part_send, part_own, part_far, first, image, result,
    load_sem, ham_sem, send_sem, recv_sem, out_sem,
):
    here = ham.shape[0]
    slots = ham.shape[1]
    block = ham.shape[2]
    side = REACH * block
    height = here * block
    width = vec.shape[2]
    last = height - side
    devices = rows_n * cols_n
    blocks_all = devices * here
    me = lax.axis_index("row") * cols_n + lax.axis_index("col")
    after = lax.rem(me + 1, devices)
    before = lax.rem(me + devices - 1, devices)
    right = (after // cols_n, lax.rem(after, cols_n))
    left = (before // cols_n, lax.rem(before, cols_n))

    barrier = pltpu.get_barrier_semaphore()
    for other in (left, right):
        pl.semaphore_signal(barrier, inc=1, device_id=other, device_id_type=MESH)

    def lanes(c):
        return pl.ds(pl.multiple_of(c * width, width), width)

    def load(c):
        return pltpu.make_async_copy(vec_hbm.at[:, lanes(c)], vec.at[c], load_sem.at[c])

    def send(kind, c):
        if kind < 2:
            src = vec.at[c, pl.ds(last * kind, side)]
        else:
            src = part_send.at[kind - 2, c]
        return pltpu.make_async_remote_copy(
            src_ref=src,
            dst_ref=halo.at[kind, c],
            send_sem=send_sem.at[kind, c],
            recv_sem=recv_sem.at[kind, c],
            device_id=left if kind % 2 == 0 else right,
            device_id_type=MESH,
        )

    def put(which, c):
        rows = ((0, side), (last, side), (side, height - 2 * side))[which]
        return pltpu.make_async_copy(
            result.at[c, pl.ds(*rows)], out_hbm.at[pl.ds(*rows), lanes(c)], out_sem.at[which, c]
        )

    @pl.loop(0, chunks)
    def _(c):
        load(c).start()

    ham_copy = pltpu.make_async_copy(ham_hbm, ham, ham_sem)
    ham_copy.start()

    @pl.loop(0, chunks)
    def _(c):
        load(c).wait()

    pl.semaphore_wait(barrier, 2)

    @pl.loop(0, chunks)
    def _(c):
        send(0, c).start()
        send(1, c).start()

    ham_copy.wait()
    band[...] = jnp.zeros_like(band)

    @pl.loop(0, here)
    def _(r):
        held = [ham[r, k].astype(F32) for k in range(slots)]
        for offset in range(2 * REACH + 1):
            place = r + offset
            target = lax.rem(me * here + place - REACH + blocks_all, blocks_all)
            total = None
            for k in range(slots):
                term = held[k] * jnp.where(columns_ref[r, k] == target, 1.0, 0.0)
                total = term if total is None else total + term
            band[
                pl.ds(pl.multiple_of(r * block, block), block),
                pl.ds(pl.multiple_of(place * block, block), block),
            ] = total.astype(BF16)

    turned[0] = band[pl.ds(0, side), pl.ds(0, side)].astype(F32).T.astype(BF16)
    turned[1] = band[pl.ds(last, side), pl.ds(height + side, side)].astype(F32).T.astype(BF16)

    low, high = bounds_ref[0], bounds_ref[1]
    center = jnp.full((1, width), 0.5 * (high + low), F32)
    inverse = 1.0 / jnp.full((1, width), 0.5 * (high - low), F32)

    top, bottom = pl.ds(0, side), pl.ds(last, side)
    middle = pl.ds(side, height - 2 * side)
    upper, lower = pl.ds(0, height - side), pl.ds(side, height - side)
    all_in = pl.ds(side, height)
    upper_in, lower_in = pl.ds(side, height - side), pl.ds(2 * side, height - side)

    @pl.loop(0, chunks)
    def _(c):
        top_part = (
            dot(band[top, upper_in], vec[c, upper]) - center * vec[c, top].astype(F32)
        ) * inverse
        part_own[0, c] = top_part
        part_send[0, c] = top_part.astype(BF16)
        bottom_part = (
            dot(band[bottom, lower_in], vec[c, lower]) - center * vec[c, bottom].astype(F32)
        ) * inverse
        part_own[1, c] = bottom_part
        part_send[1, c] = bottom_part.astype(BF16)

    @pl.loop(0, chunks)
    def _(c):
        part_far[0, c] = dot(turned[0], vec[c, top]) * inverse
        part_far[1, c] = dot(turned[1], vec[c, bottom]) * inverse
        send(2, c).start()
        send(3, c).start()
        first[c, middle] = (
            (dot(band[middle, all_in], vec[c]) - center * vec[c, middle].astype(F32)) * inverse
        ).astype(BF16)

    @pl.loop(0, chunks)
    def _(c):
        send(1, c).wait_recv()
        first[c, top] = (
            part_own[0, c] + dot(band[top, pl.ds(0, side)], halo[1, c]) * inverse
        ).astype(BF16)
        send(0, c).wait_recv()
        first[c, bottom] = (
            part_own[1, c] + dot(band[bottom, pl.ds(height + side, side)], halo[0, c]) * inverse
        ).astype(BF16)
        result[c, middle] = (
            2.0 * (
                (dot(band[middle, all_in], first[c]) - center * first[c, middle].astype(F32))
                * inverse
            )
            - vec[c, middle].astype(F32)
        ).astype(BF16)
        put(2, c).start()
        image[0, c] = dot(band[top, upper_in], first[c, upper]) - center * first[
            c, top
        ].astype(F32)
        image[1, c] = dot(band[bottom, lower_in], first[c, lower]) - center * first[
            c, bottom
        ].astype(F32)

    @pl.loop(0, chunks)
    def _(c):
        send(3, c).wait_recv()
        beyond = (halo[3, c].astype(F32) + part_far[0, c]).astype(BF16)
        result[c, top] = (
            2.0 * ((image[0, c] + dot(band[top, pl.ds(0, side)], beyond)) * inverse)
            - vec[c, top].astype(F32)
        ).astype(BF16)
        put(0, c).start()
        send(2, c).wait_recv()
        beyond = (halo[2, c].astype(F32) + part_far[1, c]).astype(BF16)
        result[c, bottom] = (
            2.0 * (
                (image[1, c] + dot(band[bottom, pl.ds(height + side, side)], beyond)) * inverse
            )
            - vec[c, bottom].astype(F32)
        ).astype(BF16)
        put(1, c).start()

    @pl.loop(0, chunks)
    def _(c):
        for kind in range(4):
            send(kind, c).wait_send()
        for which in range(3):
            put(which, c).wait()


def per_device(rows_n, cols_n, vectors, ham_blocks, ham_columns, bounds):
    height, vec_width = vectors.shape
    here, slots, block, _ = ham_blocks.shape
    side = REACH * block
    chunks = CHUNKS
    width = vec_width // chunks
    return pl.pallas_call(
        functools.partial(kernel, rows_n, cols_n, chunks),
        out_shape=jax.ShapeDtypeStruct((height, vec_width), BF16),
        in_specs=[
            pl.BlockSpec(memory_space=pltpu.SMEM),
            pl.BlockSpec(memory_space=pltpu.SMEM),
            pl.BlockSpec(memory_space=pl.ANY),
            pl.BlockSpec(memory_space=pl.ANY),
        ],
        out_specs=pl.BlockSpec(memory_space=pl.ANY),
        scratch_shapes=[
            pltpu.VMEM((here, slots, block, block), BF16),
            pltpu.VMEM((height, height + 2 * side), BF16),
            pltpu.VMEM((2, side, side), BF16),
            pltpu.VMEM((chunks, height, width), BF16),
            pltpu.VMEM((4, chunks, side, width), BF16),
            pltpu.VMEM((2, chunks, side, width), BF16),
            pltpu.VMEM((2, chunks, side, width), F32),
            pltpu.VMEM((2, chunks, side, width), F32),
            pltpu.VMEM((chunks, height, width), BF16),
            pltpu.VMEM((2, chunks, side, width), F32),
            pltpu.VMEM((chunks, height, width), BF16),
            pltpu.SemaphoreType.DMA((chunks,)),
            pltpu.SemaphoreType.DMA,
            pltpu.SemaphoreType.DMA((4, chunks)),
            pltpu.SemaphoreType.DMA((4, chunks)),
            pltpu.SemaphoreType.DMA((3, chunks)),
        ],
        compiler_params=pltpu.CompilerParams(collective_id=0, has_side_effects=True),
    )(bounds, ham_columns, vectors, ham_blocks)


def solution(mesh):
    return jax.shard_map(
        functools.partial(per_device, mesh.shape["row"], mesh.shape["col"]),
        mesh=mesh,
        in_specs=(
            P(("row", "col"), None),
            P(("row", "col"), None, None, None),
            P(("row", "col"), None),
            P(),
        ),
        out_specs=P(("row", "col"), None),
        check_vma=False,
    )
```

```python
import functools

import jax
import jax.numpy as jnp
from jax import lax
from jax.experimental import pallas as pl
from jax.experimental.pallas import tpu as pltpu
from jax.sharding import PartitionSpec as P

REACH = 2
MESH = pl.DeviceIdType.MESH
F32 = jnp.float32
BF16 = jnp.bfloat16
CHUNKS = 4
VMEM_BYTES = 20 << 20


def dot(a, b):
    return jnp.dot(a, b, preferred_element_type=F32)


def kernel(
    rows_n, cols_n, chunks,
    bounds_ref, columns_ref, vec_hbm, ham_hbm, out_ref,
    ham, band, turned, vec, halo, part_send, part_own, part_far, first, image,
    load_sem, ham_sem, send_sem, recv_sem,
):
    here = ham.shape[0]
    slots = ham.shape[1]
    block = ham.shape[2]
    side = REACH * block
    height = here * block
    width = vec.shape[2]
    last = height - side
    devices = rows_n * cols_n
    blocks_all = devices * here
    me = lax.axis_index("row") * cols_n + lax.axis_index("col")
    after = lax.rem(me + 1, devices)
    before = lax.rem(me + devices - 1, devices)
    right = (after // cols_n, lax.rem(after, cols_n))
    left = (before // cols_n, lax.rem(before, cols_n))

    barrier = pltpu.get_barrier_semaphore()
    for other in (left, right):
        pl.semaphore_signal(barrier, inc=1, device_id=other, device_id_type=MESH)

    def lanes(c):
        return pl.ds(pl.multiple_of(c * width, width), width)

    def load(c):
        return pltpu.make_async_copy(vec_hbm.at[:, lanes(c)], vec.at[c], load_sem.at[c])

    def send(kind, c):
        if kind < 2:
            src = vec_hbm.at[pl.ds(last * kind, side), lanes(c)]
        else:
            src = part_send.at[kind - 2, c]
        return pltpu.make_async_remote_copy(
            src_ref=src,
            dst_ref=halo.at[kind, c],
            send_sem=send_sem.at[kind, c],
            recv_sem=recv_sem.at[kind, c],
            device_id=left if kind % 2 == 0 else right,
            device_id_type=MESH,
        )

    ham_copy = pltpu.make_async_copy(ham_hbm, ham, ham_sem)
    ham_copy.start()

    @pl.loop(0, chunks)
    def _(c):
        load(c).start()

    pl.semaphore_wait(barrier, 2)

    @pl.loop(0, chunks)
    def _(c):
        send(0, c).start()
        send(1, c).start()

    ham_copy.wait()
    band[...] = jnp.zeros_like(band)

    @pl.loop(0, here)
    def _(r):
        held = [ham[r, k].astype(F32) for k in range(slots)]
        for offset in range(2 * REACH + 1):
            place = r + offset
            target = lax.rem(me * here + place - REACH + blocks_all, blocks_all)
            total = None
            for k in range(slots):
                term = held[k] * jnp.where(columns_ref[r, k] == target, 1.0, 0.0)
                total = term if total is None else total + term
            band[
                pl.ds(pl.multiple_of(r * block, block), block),
                pl.ds(pl.multiple_of(place * block, block), block),
            ] = total.astype(BF16)

    turned[0] = band[pl.ds(0, side), pl.ds(0, side)].astype(F32).T.astype(BF16)
    turned[1] = band[pl.ds(last, side), pl.ds(height + side, side)].astype(F32).T.astype(BF16)

    low, high = bounds_ref[0], bounds_ref[1]
    center = jnp.full((1, width), 0.5 * (high + low), F32)
    inverse = 1.0 / jnp.full((1, width), 0.5 * (high - low), F32)

    top, bottom = pl.ds(0, side), pl.ds(last, side)
    middle = pl.ds(side, height - 2 * side)
    upper, lower = pl.ds(0, height - side), pl.ds(side, height - side)
    all_in = pl.ds(side, height)
    upper_in, lower_in = pl.ds(side, height - side), pl.ds(2 * side, height - side)

    @pl.loop(0, chunks)
    def _(c):
        load(c).wait()
        top_part = (
            dot(band[top, upper_in], vec[c, upper]) - center * vec[c, top].astype(F32)
        ) * inverse
        part_own[0, c] = top_part
        part_send[0, c] = top_part.astype(BF16)
        bottom_part = (
            dot(band[bottom, lower_in], vec[c, lower]) - center * vec[c, bottom].astype(F32)
        ) * inverse
        part_own[1, c] = bottom_part
        part_send[1, c] = bottom_part.astype(BF16)

    @pl.loop(0, chunks)
    def _(c):
        part_far[0, c] = dot(turned[0], vec[c, top]) * inverse
        part_far[1, c] = dot(turned[1], vec[c, bottom]) * inverse
        send(2, c).start()
        send(3, c).start()
        first[c, middle] = (
            (dot(band[middle, all_in], vec[c]) - center * vec[c, middle].astype(F32)) * inverse
        ).astype(BF16)

    @pl.loop(0, chunks)
    def _(c):
        send(1, c).wait_recv()
        first[c, top] = (
            part_own[0, c] + dot(band[top, pl.ds(0, side)], halo[1, c]) * inverse
        ).astype(BF16)
        send(0, c).wait_recv()
        first[c, bottom] = (
            part_own[1, c] + dot(band[bottom, pl.ds(height + side, side)], halo[0, c]) * inverse
        ).astype(BF16)
        out_ref[middle, lanes(c)] = (
            2.0 * (
                (dot(band[middle, all_in], first[c]) - center * first[c, middle].astype(F32))
                * inverse
            )
            - vec[c, middle].astype(F32)
        ).astype(BF16)
        image[0, c] = dot(band[top, upper_in], first[c, upper]) - center * first[
            c, top
        ].astype(F32)
        image[1, c] = dot(band[bottom, lower_in], first[c, lower]) - center * first[
            c, bottom
        ].astype(F32)

    @pl.loop(0, chunks)
    def _(c):
        send(3, c).wait_recv()
        beyond = (halo[3, c].astype(F32) + part_far[0, c]).astype(BF16)
        out_ref[top, lanes(c)] = (
            2.0 * ((image[0, c] + dot(band[top, pl.ds(0, side)], beyond)) * inverse)
            - vec[c, top].astype(F32)
        ).astype(BF16)
        send(2, c).wait_recv()
        beyond = (halo[2, c].astype(F32) + part_far[1, c]).astype(BF16)
        out_ref[bottom, lanes(c)] = (
            2.0 * (
                (image[1, c] + dot(band[bottom, pl.ds(height + side, side)], beyond)) * inverse
            )
            - vec[c, bottom].astype(F32)
        ).astype(BF16)

    @pl.loop(0, chunks)
    def _(c):
        for kind in range(4):
            send(kind, c).wait_send()


def per_device(rows_n, cols_n, vectors, ham_blocks, ham_columns, bounds):
    height, vec_width = vectors.shape
    here, slots, block, _ = ham_blocks.shape
    side = REACH * block
    chunks = CHUNKS
    width = vec_width // chunks
    return pl.pallas_call(
        functools.partial(kernel, rows_n, cols_n, chunks),
        out_shape=jax.ShapeDtypeStruct((height, vec_width), BF16),
        in_specs=[
            pl.BlockSpec(memory_space=pltpu.SMEM),
            pl.BlockSpec(memory_space=pltpu.SMEM),
            pl.BlockSpec(memory_space=pltpu.HBM),
            pl.BlockSpec(memory_space=pltpu.HBM),
        ],
        out_specs=pl.BlockSpec(memory_space=pltpu.VMEM),
        scratch_shapes=[
            pltpu.VMEM((here, slots, block, block), BF16),
            pltpu.VMEM((height, height + 2 * side), BF16),
            pltpu.VMEM((2, side, side), BF16),
            pltpu.VMEM((chunks, height, width), BF16),
            pltpu.VMEM((4, chunks, side, width), BF16),
            pltpu.VMEM((2, chunks, side, width), BF16),
            pltpu.VMEM((2, chunks, side, width), F32),
            pltpu.VMEM((2, chunks, side, width), F32),
            pltpu.VMEM((chunks, height, width), BF16),
            pltpu.VMEM((2, chunks, side, width), F32),
            pltpu.SemaphoreType.DMA((chunks,)),
            pltpu.SemaphoreType.DMA,
            pltpu.SemaphoreType.DMA((4, chunks)),
            pltpu.SemaphoreType.DMA((4, chunks)),
        ],
        compiler_params=pltpu.CompilerParams(
            collective_id=0, has_side_effects=True, vmem_limit_bytes=VMEM_BYTES
        ),
    )(*[pltpu.with_memory_space_constraint(a, pltpu.HBM) for a in (bounds, ham_columns, vectors, ham_blocks)])


def solution(mesh):
    return jax.shard_map(
        functools.partial(per_device, mesh.shape["row"], mesh.shape["col"]),
        mesh=mesh,
        in_specs=(
            P(("row", "col"), None),
            P(("row", "col"), None, None, None),
            P(("row", "col"), None),
            P(),
        ),
        out_specs=P(("row", "col"), None),
        check_vma=False,
    )
```

```python
import functools

import jax
import jax.numpy as jnp
from jax import lax
from jax.experimental import pallas as pl
from jax.experimental.pallas import tpu as pltpu
from jax.sharding import PartitionSpec as P

REACH = 2
MESH = pl.DeviceIdType.MESH
F32 = jnp.float32
BF16 = jnp.bfloat16
CHUNKS = 4
VMEM_BYTES = 20 << 20


def dot(a, b):
    return jnp.dot(a, b, preferred_element_type=F32)


def kernel(
    rows_n, cols_n, chunks,
    bounds_hbm, columns_hbm, vec_hbm, ham_hbm, out_ref,
    bounds_ref, columns_ref, ham, band, turned, vec, halo, part_send, part_own, part_far, first, image,
    load_sem, ham_sem, small_sem, send_sem, recv_sem,
):
    here = ham.shape[0]
    slots = ham.shape[1]
    block = ham.shape[2]
    side = REACH * block
    height = here * block
    width = vec.shape[2]
    last = height - side
    devices = rows_n * cols_n
    blocks_all = devices * here
    me = lax.axis_index("row") * cols_n + lax.axis_index("col")
    after = lax.rem(me + 1, devices)
    before = lax.rem(me + devices - 1, devices)
    right = (after // cols_n, lax.rem(after, cols_n))
    left = (before // cols_n, lax.rem(before, cols_n))

    barrier = pltpu.get_barrier_semaphore()
    for other in (left, right):
        pl.semaphore_signal(barrier, inc=1, device_id=other, device_id_type=MESH)

    def lanes(c):
        return pl.ds(pl.multiple_of(c * width, width), width)

    def load(c):
        return pltpu.make_async_copy(vec_hbm.at[:, lanes(c)], vec.at[c], load_sem.at[c])

    def send(kind, c):
        if kind < 2:
            src = vec_hbm.at[pl.ds(last * kind, side), lanes(c)]
        else:
            src = part_send.at[kind - 2, c]
        return pltpu.make_async_remote_copy(
            src_ref=src,
            dst_ref=halo.at[kind, c],
            send_sem=send_sem.at[kind, c],
            recv_sem=recv_sem.at[kind, c],
            device_id=left if kind % 2 == 0 else right,
            device_id_type=MESH,
        )

    small = [
        pltpu.make_async_copy(columns_hbm, columns_ref, small_sem.at[0]),
        pltpu.make_async_copy(bounds_hbm, bounds_ref, small_sem.at[1]),
    ]
    for copy in small:
        copy.start()
    ham_copy = pltpu.make_async_copy(ham_hbm, ham, ham_sem)
    ham_copy.start()

    @pl.loop(0, chunks)
    def _(c):
        load(c).start()

    pl.semaphore_wait(barrier, 2)

    @pl.loop(0, chunks)
    def _(c):
        send(0, c).start()
        send(1, c).start()

    for copy in small:
        copy.wait()
    ham_copy.wait()
    band[...] = jnp.zeros_like(band)

    @pl.loop(0, here)
    def _(r):
        held = [ham[r, k].astype(F32) for k in range(slots)]
        for offset in range(2 * REACH + 1):
            place = r + offset
            target = lax.rem(me * here + place - REACH + blocks_all, blocks_all)
            total = None
            for k in range(slots):
                term = held[k] * jnp.where(columns_ref[r, k] == target, 1.0, 0.0)
                total = term if total is None else total + term
            band[
                pl.ds(pl.multiple_of(r * block, block), block),
                pl.ds(pl.multiple_of(place * block, block), block),
            ] = total.astype(BF16)

    turned[0] = band[pl.ds(0, side), pl.ds(0, side)].astype(F32).T.astype(BF16)
    turned[1] = band[pl.ds(last, side), pl.ds(height + side, side)].astype(F32).T.astype(BF16)

    low, high = bounds_ref[0], bounds_ref[1]
    center = jnp.full((1, width), 0.5 * (high + low), F32)
    inverse = 1.0 / jnp.full((1, width), 0.5 * (high - low), F32)
    double = 2.0 * inverse

    top, bottom = pl.ds(0, side), pl.ds(last, side)
    middle = pl.ds(side, height - 2 * side)
    upper, lower = pl.ds(0, height - side), pl.ds(side, height - side)
    all_in = pl.ds(side, height)
    upper_in, lower_in = pl.ds(side, height - side), pl.ds(2 * side, height - side)

    @pl.loop(0, chunks)
    def _(c):
        load(c).wait()
        top_part = (
            dot(band[top, upper_in], vec[c, upper]) - center * vec[c, top].astype(F32)
        ) * inverse
        part_own[0, c] = top_part
        part_send[0, c] = top_part.astype(BF16)
        bottom_part = (
            dot(band[bottom, lower_in], vec[c, lower]) - center * vec[c, bottom].astype(F32)
        ) * inverse
        part_own[1, c] = bottom_part
        part_send[1, c] = bottom_part.astype(BF16)

    @pl.loop(0, chunks)
    def _(c):
        part_far[0, c] = dot(turned[0], vec[c, top]) * inverse
        part_far[1, c] = dot(turned[1], vec[c, bottom]) * inverse
        send(2, c).start()
        send(3, c).start()
        first[c, middle] = (
            (dot(band[middle, all_in], vec[c]) - center * vec[c, middle].astype(F32)) * inverse
        ).astype(BF16)

    @pl.loop(0, chunks)
    def _(c):
        send(1, c).wait_recv()
        first[c, top] = (
            part_own[0, c] + dot(band[top, pl.ds(0, side)], halo[1, c]) * inverse
        ).astype(BF16)
        send(0, c).wait_recv()
        first[c, bottom] = (
            part_own[1, c] + dot(band[bottom, pl.ds(height + side, side)], halo[0, c]) * inverse
        ).astype(BF16)
        out_ref[middle, lanes(c)] = (
            (dot(band[middle, all_in], first[c]) - center * first[c, middle].astype(F32)) * double
            - vec[c, middle].astype(F32)
        ).astype(BF16)
        image[0, c] = (
            dot(band[top, upper_in], first[c, upper]) - center * first[c, top].astype(F32)
        ) * double - vec[c, top].astype(F32)
        image[1, c] = (
            dot(band[bottom, lower_in], first[c, lower]) - center * first[c, bottom].astype(F32)
        ) * double - vec[c, bottom].astype(F32)

    @pl.loop(0, chunks)
    def _(c):
        send(2, c).wait_recv()
        beyond = (halo[2, c].astype(F32) + part_far[1, c]).astype(BF16)
        out_ref[bottom, lanes(c)] = (
            image[1, c] + dot(band[bottom, pl.ds(height + side, side)], beyond) * double
        ).astype(BF16)
        send(3, c).wait_recv()
        beyond = (halo[3, c].astype(F32) + part_far[0, c]).astype(BF16)
        out_ref[top, lanes(c)] = (
            image[0, c] + dot(band[top, pl.ds(0, side)], beyond) * double
        ).astype(BF16)

    @pl.loop(0, chunks)
    def _(c):
        for kind in range(4):
            send(kind, c).wait_send()


def per_device(rows_n, cols_n, vectors, ham_blocks, ham_columns, bounds):
    height, vec_width = vectors.shape
    here, slots, block, _ = ham_blocks.shape
    side = REACH * block
    chunks = CHUNKS
    width = vec_width // chunks
    return pl.pallas_call(
        functools.partial(kernel, rows_n, cols_n, chunks),
        out_shape=jax.ShapeDtypeStruct((height, vec_width), BF16),
        in_specs=[
            pl.BlockSpec(memory_space=pltpu.HBM),
            pl.BlockSpec(memory_space=pltpu.HBM),
            pl.BlockSpec(memory_space=pltpu.HBM),
            pl.BlockSpec(memory_space=pltpu.HBM),
        ],
        out_specs=pl.BlockSpec(memory_space=pltpu.VMEM),
        scratch_shapes=[
            pltpu.SMEM(bounds.shape, F32),
            pltpu.SMEM(ham_columns.shape, jnp.int32),
            pltpu.VMEM((here, slots, block, block), BF16),
            pltpu.VMEM((height, height + 2 * side), BF16),
            pltpu.VMEM((2, side, side), BF16),
            pltpu.VMEM((chunks, height, width), BF16),
            pltpu.VMEM((4, chunks, side, width), BF16),
            pltpu.VMEM((2, chunks, side, width), BF16),
            pltpu.VMEM((2, chunks, side, width), F32),
            pltpu.VMEM((2, chunks, side, width), F32),
            pltpu.VMEM((chunks, height, width), BF16),
            pltpu.VMEM((2, chunks, side, width), F32),
            pltpu.SemaphoreType.DMA((chunks,)),
            pltpu.SemaphoreType.DMA,
            pltpu.SemaphoreType.DMA((2,)),
            pltpu.SemaphoreType.DMA((4, chunks)),
            pltpu.SemaphoreType.DMA((4, chunks)),
        ],
        compiler_params=pltpu.CompilerParams(
            collective_id=0, has_side_effects=True, vmem_limit_bytes=VMEM_BYTES
        ),
    )(*[pltpu.with_memory_space_constraint(a, pltpu.HBM) for a in (bounds, ham_columns, vectors, ham_blocks)])


def solution(mesh):
    return jax.shard_map(
        functools.partial(per_device, mesh.shape["row"], mesh.shape["col"]),
        mesh=mesh,
        in_specs=(
            P(("row", "col"), None),
            P(("row", "col"), None, None, None),
            P(("row", "col"), None),
            P(),
        ),
        out_specs=P(("row", "col"), None),
        check_vma=False,
    )
```

```python
import functools

import jax
import jax.numpy as jnp
from jax import lax
from jax.experimental import pallas as pl
from jax.experimental.pallas import tpu as pltpu
from jax.sharding import PartitionSpec as P

REACH = 2
MESH = pl.DeviceIdType.MESH
F32 = jnp.float32
BF16 = jnp.bfloat16
CHUNKS = 4
VMEM_BYTES = 20 << 20


def dot(a, b):
    return jnp.dot(a, b, preferred_element_type=F32)


def kernel(
    rows_n, cols_n, chunks,
    bounds_hbm, columns_hbm, vec_hbm, ham_hbm, out_ref,
    bounds_ref, columns_ref, ham, band, turned, vec, halo, part_send, part_own, part_far, first, image,
    load_sem, ham_sem, small_sem, ready_sem, send_sem, recv_sem,
):
    here = ham.shape[0]
    slots = ham.shape[1]
    block = ham.shape[2]
    side = REACH * block
    height = here * block
    width = vec.shape[2]
    last = height - side
    devices = rows_n * cols_n
    blocks_all = devices * here
    me = lax.axis_index("row") * cols_n + lax.axis_index("col")
    after = lax.rem(me + 1, devices)
    before = lax.rem(me + devices - 1, devices)
    right = (after // cols_n, lax.rem(after, cols_n))
    left = (before // cols_n, lax.rem(before, cols_n))

    barrier = pltpu.get_barrier_semaphore()
    pl.semaphore_signal(barrier, inc=1, device_id=left, device_id_type=MESH)

    def lanes(c):
        return pl.ds(pl.multiple_of(c * width, width), width)

    def load(c):
        return pltpu.make_async_copy(vec_hbm.at[:, lanes(c)], vec.at[c], load_sem.at[c])

    def send(kind, c):
        if kind < 2:
            src = vec_hbm.at[pl.ds(last * kind, side), lanes(c)]
        else:
            src = part_send.at[kind - 2, c]
        return pltpu.make_async_remote_copy(
            src_ref=src,
            dst_ref=halo.at[kind, c],
            send_sem=send_sem.at[kind, c],
            recv_sem=recv_sem.at[kind, c],
            device_id=left if kind % 2 == 0 else right,
            device_id_type=MESH,
        )

    pl.semaphore_wait(barrier, 1)

    @pl.loop(0, chunks)
    def _(c):
        send(1, c).start()

    pl.semaphore_signal(ready_sem, inc=1, device_id=right, device_id_type=MESH)

    small = [
        pltpu.make_async_copy(columns_hbm, columns_ref, small_sem.at[0]),
        pltpu.make_async_copy(bounds_hbm, bounds_ref, small_sem.at[1]),
    ]
    for copy in small:
        copy.start()
    ham_copy = pltpu.make_async_copy(ham_hbm, ham, ham_sem)
    ham_copy.start()

    @pl.loop(0, chunks)
    def _(c):
        load(c).start()

    pl.semaphore_wait(ready_sem, 1)

    @pl.loop(0, chunks)
    def _(c):
        send(0, c).start()

    for copy in small:
        copy.wait()
    ham_copy.wait()
    band[...] = jnp.zeros_like(band)

    @pl.loop(0, here)
    def _(r):
        held = [ham[r, k].astype(F32) for k in range(slots)]
        for offset in range(2 * REACH + 1):
            place = r + offset
            target = lax.rem(me * here + place - REACH + blocks_all, blocks_all)
            total = None
            for k in range(slots):
                term = held[k] * jnp.where(columns_ref[r, k] == target, 1.0, 0.0)
                total = term if total is None else total + term
            band[
                pl.ds(pl.multiple_of(r * block, block), block),
                pl.ds(pl.multiple_of(place * block, block), block),
            ] = total.astype(BF16)

    turned[0] = band[pl.ds(0, side), pl.ds(0, side)].astype(F32).T.astype(BF16)
    turned[1] = band[pl.ds(last, side), pl.ds(height + side, side)].astype(F32).T.astype(BF16)

    low, high = bounds_ref[0], bounds_ref[1]
    center = jnp.full((1, width), 0.5 * (high + low), F32)
    inverse = 1.0 / jnp.full((1, width), 0.5 * (high - low), F32)
    double = 2.0 * inverse

    top, bottom = pl.ds(0, side), pl.ds(last, side)
    middle = pl.ds(side, height - 2 * side)
    upper, lower = pl.ds(0, height - side), pl.ds(side, height - side)
    all_in = pl.ds(side, height)
    upper_in, lower_in = pl.ds(side, height - side), pl.ds(2 * side, height - side)

    @pl.loop(0, chunks)
    def _(c):
        load(c).wait()
        top_part = (
            dot(band[top, upper_in], vec[c, upper]) - center * vec[c, top].astype(F32)
        ) * inverse
        part_own[0, c] = top_part
        part_send[0, c] = top_part.astype(BF16)
        bottom_part = (
            dot(band[bottom, lower_in], vec[c, lower]) - center * vec[c, bottom].astype(F32)
        ) * inverse
        part_own[1, c] = bottom_part
        part_send[1, c] = bottom_part.astype(BF16)

    @pl.loop(0, chunks)
    def _(c):
        part_far[0, c] = dot(turned[0], vec[c, top]) * inverse
        part_far[1, c] = dot(turned[1], vec[c, bottom]) * inverse
        send(2, c).start()
        send(3, c).start()
        first[c, middle] = (
            (dot(band[middle, all_in], vec[c]) - center * vec[c, middle].astype(F32)) * inverse
        ).astype(BF16)

    @pl.loop(0, chunks)
    def _(c):
        send(1, c).wait_recv()
        first[c, top] = (
            part_own[0, c] + dot(band[top, pl.ds(0, side)], halo[1, c]) * inverse
        ).astype(BF16)
        send(0, c).wait_recv()
        first[c, bottom] = (
            part_own[1, c] + dot(band[bottom, pl.ds(height + side, side)], halo[0, c]) * inverse
        ).astype(BF16)
        out_ref[middle, lanes(c)] = (
            (dot(band[middle, all_in], first[c]) - center * first[c, middle].astype(F32)) * double
            - vec[c, middle].astype(F32)
        ).astype(BF16)
        image[0, c] = (
            dot(band[top, upper_in], first[c, upper]) - center * first[c, top].astype(F32)
        ) * double - vec[c, top].astype(F32)
        image[1, c] = (
            dot(band[bottom, lower_in], first[c, lower]) - center * first[c, bottom].astype(F32)
        ) * double - vec[c, bottom].astype(F32)

    @pl.loop(0, chunks)
    def _(c):
        send(2, c).wait_recv()
        beyond = (halo[2, c].astype(F32) + part_far[1, c]).astype(BF16)
        out_ref[bottom, lanes(c)] = (
            image[1, c] + dot(band[bottom, pl.ds(height + side, side)], beyond) * double
        ).astype(BF16)
        send(3, c).wait_recv()
        beyond = (halo[3, c].astype(F32) + part_far[0, c]).astype(BF16)
        out_ref[top, lanes(c)] = (
            image[0, c] + dot(band[top, pl.ds(0, side)], beyond) * double
        ).astype(BF16)

    @pl.loop(0, chunks)
    def _(c):
        for kind in range(4):
            send(kind, c).wait_send()


def per_device(rows_n, cols_n, vectors, ham_blocks, ham_columns, bounds):
    height, vec_width = vectors.shape
    here, slots, block, _ = ham_blocks.shape
    side = REACH * block
    chunks = CHUNKS
    width = vec_width // chunks
    return pl.pallas_call(
        functools.partial(kernel, rows_n, cols_n, chunks),
        out_shape=jax.ShapeDtypeStruct((height, vec_width), BF16),
        in_specs=[
            pl.BlockSpec(memory_space=pltpu.HBM),
            pl.BlockSpec(memory_space=pltpu.HBM),
            pl.BlockSpec(memory_space=pltpu.HBM),
            pl.BlockSpec(memory_space=pltpu.HBM),
        ],
        out_specs=pl.BlockSpec(memory_space=pltpu.VMEM),
        scratch_shapes=[
            pltpu.SMEM(bounds.shape, F32),
            pltpu.SMEM(ham_columns.shape, jnp.int32),
            pltpu.VMEM((here, slots, block, block), BF16),
            pltpu.VMEM((height, height + 2 * side), BF16),
            pltpu.VMEM((2, side, side), BF16),
            pltpu.VMEM((chunks, height, width), BF16),
            pltpu.VMEM((4, chunks, side, width), BF16),
            pltpu.VMEM((2, chunks, side, width), BF16),
            pltpu.VMEM((2, chunks, side, width), F32),
            pltpu.VMEM((2, chunks, side, width), F32),
            pltpu.VMEM((chunks, height, width), BF16),
            pltpu.VMEM((2, chunks, side, width), F32),
            pltpu.SemaphoreType.DMA((chunks,)),
            pltpu.SemaphoreType.DMA,
            pltpu.SemaphoreType.DMA((2,)),
            pltpu.SemaphoreType.REGULAR,
            pltpu.SemaphoreType.DMA((4, chunks)),
            pltpu.SemaphoreType.DMA((4, chunks)),
        ],
        compiler_params=pltpu.CompilerParams(
            collective_id=0, has_side_effects=True, vmem_limit_bytes=VMEM_BYTES
        ),
    )(*[pltpu.with_memory_space_constraint(a, pltpu.HBM) for a in (bounds, ham_columns, vectors, ham_blocks)])


def solution(mesh):
    return jax.shard_map(
        functools.partial(per_device, mesh.shape["row"], mesh.shape["col"]),
        mesh=mesh,
        in_specs=(
            P(("row", "col"), None),
            P(("row", "col"), None, None, None),
            P(("row", "col"), None),
            P(),
        ),
        out_specs=P(("row", "col"), None),
        check_vma=False,
    )
```

```python
import functools

import jax
import jax.numpy as jnp
from jax import lax
from jax.experimental import pallas as pl
from jax.experimental.pallas import tpu as pltpu
from jax.sharding import PartitionSpec as P

REACH = 2
MESH = pl.DeviceIdType.MESH
F32 = jnp.float32
BF16 = jnp.bfloat16
CHUNKS = 4
VECTOR_PIECES = 1
PIECES = (1, 1, 1, 1)
VMEM_BYTES = 20 << 20


def dot(a, b):
    return jnp.dot(a, b, preferred_element_type=F32)


def kernel(
    rows_n, cols_n, chunks, vector_pieces, partial_pieces,
    bounds_hbm, columns_hbm, vec_hbm, ham_hbm, out_ref,
    bounds_ref, columns_ref, ham, band, turned, vec, halo, part_halo, part_send, part_own, part_far, first, image,
    load_sem, ham_sem, small_sem, ready_sem, turn_sem,
    vec_send_sem, vec_recv_sem, part_send_sem, part_recv_sem,
):
    here = ham.shape[0]
    slots = ham.shape[1]
    block = ham.shape[2]
    side = REACH * block
    height = here * block
    width = vec.shape[2]
    total_width = chunks * width
    last = height - side
    devices = rows_n * cols_n
    blocks_all = devices * here
    me = lax.axis_index("row") * cols_n + lax.axis_index("col")
    after = lax.rem(me + 1, devices)
    before = lax.rem(me + devices - 1, devices)
    right = (after // cols_n, lax.rem(after, cols_n))
    left = (before // cols_n, lax.rem(before, cols_n))

    row, col = lax.axis_index("row"), lax.axis_index("col")
    run = cols_n // 2
    core = lax.rem(row, 2)
    far = lax.rem(row // 2, 2) * (col // run)
    at_end = (lax.rem(col, run) == run - 1).astype(jnp.int32)
    leads = at_end * (1 - lax.rem(core + far, 2))
    follows = at_end - leads
    partner = (row + 1 - 2 * core, col)

    turn = len(partial_pieces) // 2

    barrier = pltpu.get_barrier_semaphore()
    pl.semaphore_signal(barrier, inc=1, device_id=left, device_id_type=MESH)

    @pl.when(follows == 1)
    def _():
        pl.semaphore_signal(barrier, inc=1, device_id=partner, device_id_type=MESH)


    def lanes(c):
        return pl.ds(pl.multiple_of(c * width, width), width)

    def load(c):
        return pltpu.make_async_copy(vec_hbm.at[:, lanes(c)], vec.at[c], load_sem.at[c])

    def send_vectors(kind, k):
        part = pl.ds(k * (total_width // vector_pieces), total_width // vector_pieces)
        return pltpu.make_async_remote_copy(
            src_ref=vec_hbm.at[pl.ds(last * kind, side), part],
            dst_ref=halo.at[kind, :, part],
            send_sem=vec_send_sem.at[kind, k],
            recv_sem=vec_recv_sem.at[kind, k],
            device_id=(left, right)[kind],
            device_id_type=MESH,
        )

    def send_partial(kind, k):
        part = pl.ds(*partial_pieces[k])
        return pltpu.make_async_remote_copy(
            src_ref=part_send.at[kind, :, part],
            dst_ref=part_halo.at[kind, :, part],
            send_sem=part_send_sem.at[kind, k],
            recv_sem=part_recv_sem.at[kind, k],
            device_id=(left, right)[kind],
            device_id_type=MESH,
        )

    pl.semaphore_wait(barrier, 1 + leads)

    for k in range(vector_pieces):
        send_vectors(1, k).start()

    pl.semaphore_signal(ready_sem, inc=1, device_id=right, device_id_type=MESH)

    small = [
        pltpu.make_async_copy(columns_hbm, columns_ref, small_sem.at[0]),
        pltpu.make_async_copy(bounds_hbm, bounds_ref, small_sem.at[1]),
    ]
    for copy in small:
        copy.start()
    ham_copy = pltpu.make_async_copy(ham_hbm, ham, ham_sem)
    ham_copy.start()

    @pl.loop(0, chunks)
    def _(c):
        load(c).start()

    pl.semaphore_wait(ready_sem, 1)

    for k in range(vector_pieces):
        send_vectors(0, k).start()

    for copy in small:
        copy.wait()
    ham_copy.wait()
    band[...] = jnp.zeros_like(band)

    @pl.loop(0, here)
    def _(r):
        held = [ham[r, k].astype(F32) for k in range(slots)]
        for offset in range(2 * REACH + 1):
            place = r + offset
            target = lax.rem(me * here + place - REACH + blocks_all, blocks_all)
            total = None
            for k in range(slots):
                term = held[k] * jnp.where(columns_ref[r, k] == target, 1.0, 0.0)
                total = term if total is None else total + term
            band[
                pl.ds(pl.multiple_of(r * block, block), block),
                pl.ds(pl.multiple_of(place * block, block), block),
            ] = total.astype(BF16)

    turned[0] = band[pl.ds(0, side), pl.ds(0, side)].astype(F32).T.astype(BF16)
    turned[1] = band[pl.ds(last, side), pl.ds(height + side, side)].astype(F32).T.astype(BF16)

    low, high = bounds_ref[0], bounds_ref[1]
    center = jnp.full((1, width), 0.5 * (high + low), F32)
    inverse = 1.0 / jnp.full((1, width), 0.5 * (high - low), F32)
    double = 2.0 * inverse

    top, bottom = pl.ds(0, side), pl.ds(last, side)
    middle = pl.ds(side, height - 2 * side)
    upper, lower = pl.ds(0, height - side), pl.ds(side, height - side)
    all_in = pl.ds(side, height)
    upper_in, lower_in = pl.ds(side, height - side), pl.ds(2 * side, height - side)

    @pl.loop(0, chunks)
    def _(c):
        load(c).wait()
        top_part = (
            dot(band[top, upper_in], vec[c, upper]) - center * vec[c, top].astype(F32)
        ) * inverse
        part_own[0, c] = top_part
        part_send[0, :, lanes(c)] = top_part.astype(BF16)
        bottom_part = (
            dot(band[bottom, lower_in], vec[c, lower]) - center * vec[c, bottom].astype(F32)
        ) * inverse
        part_own[1, c] = bottom_part
        part_send[1, :, lanes(c)] = bottom_part.astype(BF16)

    @pl.loop(0, chunks)
    def _(c):
        part_far[0, :, lanes(c)] = dot(turned[0], vec[c, top]) * inverse
        part_far[1, :, lanes(c)] = dot(turned[1], vec[c, bottom]) * inverse

    for k in range(len(partial_pieces)):
        send_partial(0, k).start()

    @pl.when(follows == 0)
    def _():
        for k in range(len(partial_pieces)):
            send_partial(1, k).start()

    @pl.loop(0, chunks)
    def _(c):
        first[c, middle] = (
            (dot(band[middle, all_in], vec[c]) - center * vec[c, middle].astype(F32)) * inverse
        ).astype(BF16)

    @pl.when(leads == 1)
    def _():
        for k in range(turn):
            send_partial(1, k).wait_send()
        pl.semaphore_signal(turn_sem, inc=1, device_id=partner, device_id_type=MESH)

    @pl.when(follows == 1)
    def _():
        pl.semaphore_wait(turn_sem, 1)
        for k in range(len(partial_pieces)):
            send_partial(1, k).start()

    def second(c):
        first[c, top] = (
            part_own[0, c] + dot(band[top, pl.ds(0, side)], halo[1, :, lanes(c)]) * inverse
        ).astype(BF16)
        first[c, bottom] = (
            part_own[1, c]
            + dot(band[bottom, pl.ds(height + side, side)], halo[0, :, lanes(c)]) * inverse
        ).astype(BF16)
        out_ref[middle, lanes(c)] = (
            (dot(band[middle, all_in], first[c]) - center * first[c, middle].astype(F32)) * double
            - vec[c, middle].astype(F32)
        ).astype(BF16)
        image[0, :, lanes(c)] = (
            dot(band[top, upper_in], first[c, upper]) - center * first[c, top].astype(F32)
        ) * double - vec[c, top].astype(F32)
        image[1, :, lanes(c)] = (
            dot(band[bottom, lower_in], first[c, lower]) - center * first[c, bottom].astype(F32)
        ) * double - vec[c, bottom].astype(F32)

    for k in range(vector_pieces):
        send_vectors(0, k).wait_recv()
        send_vectors(1, k).wait_recv()
        pl.loop(k * chunks // vector_pieces, (k + 1) * chunks // vector_pieces)(second)

    for k, piece in enumerate(partial_pieces):
        part = pl.ds(*piece)
        scale = jnp.broadcast_to(double[:, :1], (1, piece[1]))
        for kind, rows, beside in (
            (0, bottom, pl.ds(height + side, side)),
            (1, top, pl.ds(0, side)),
        ):
            send_partial(kind, k).wait_recv()
            beyond = part_halo[kind, :, part].astype(F32) + part_far[1 - kind, :, part]
            out_ref[rows, part] = (
                image[1 - kind, :, part] + dot(band[rows, beside], beyond.astype(BF16)) * scale
            ).astype(BF16)

    @pl.when(leads == 0)
    def _():
        for k in range(turn):
            send_partial(1, k).wait_send()

    for k in range(turn, len(partial_pieces)):
        send_partial(1, k).wait_send()
    for k in range(len(partial_pieces)):
        send_partial(0, k).wait_send()
    for kind in range(2):
        for k in range(vector_pieces):
            send_vectors(kind, k).wait_send()


def per_device(rows_n, cols_n, vectors, ham_blocks, ham_columns, bounds):
    height, vec_width = vectors.shape
    here, slots, block, _ = ham_blocks.shape
    side = REACH * block
    chunks = CHUNKS
    width = vec_width // chunks
    pieces = []
    for share in PIECES:
        start = sum(size for _, size in pieces)
        pieces.append((start, vec_width * share // sum(PIECES)))
    return pl.pallas_call(
        functools.partial(kernel, rows_n, cols_n, chunks, VECTOR_PIECES, tuple(pieces)),
        out_shape=jax.ShapeDtypeStruct((height, vec_width), BF16),
        in_specs=[
            pl.BlockSpec(memory_space=pltpu.HBM),
            pl.BlockSpec(memory_space=pltpu.HBM),
            pl.BlockSpec(memory_space=pltpu.HBM),
            pl.BlockSpec(memory_space=pltpu.HBM),
        ],
        out_specs=pl.BlockSpec(memory_space=pltpu.VMEM),
        scratch_shapes=[
            pltpu.SMEM(bounds.shape, F32),
            pltpu.SMEM(ham_columns.shape, jnp.int32),
            pltpu.VMEM((here, slots, block, block), BF16),
            pltpu.VMEM((height, height + 2 * side), BF16),
            pltpu.VMEM((2, side, side), BF16),
            pltpu.VMEM((chunks, height, width), BF16),
            pltpu.VMEM((2, side, vec_width), BF16),
            pltpu.VMEM((2, side, vec_width), BF16),
            pltpu.VMEM((2, side, vec_width), BF16),
            pltpu.VMEM((2, chunks, side, width), F32),
            pltpu.VMEM((2, side, vec_width), F32),
            pltpu.VMEM((chunks, height, width), BF16),
            pltpu.VMEM((2, side, vec_width), F32),
            pltpu.SemaphoreType.DMA((chunks,)),
            pltpu.SemaphoreType.DMA,
            pltpu.SemaphoreType.DMA((2,)),
            pltpu.SemaphoreType.REGULAR,
            pltpu.SemaphoreType.REGULAR,
            pltpu.SemaphoreType.DMA((2, VECTOR_PIECES)),
            pltpu.SemaphoreType.DMA((2, VECTOR_PIECES)),
            pltpu.SemaphoreType.DMA((2, len(pieces))),
            pltpu.SemaphoreType.DMA((2, len(pieces))),
        ],
        compiler_params=pltpu.CompilerParams(
            collective_id=0, has_side_effects=True, vmem_limit_bytes=VMEM_BYTES
        ),
    )(*[pltpu.with_memory_space_constraint(a, pltpu.HBM) for a in (bounds, ham_columns, vectors, ham_blocks)])


def solution(mesh):
    return jax.shard_map(
        functools.partial(per_device, mesh.shape["row"], mesh.shape["col"]),
        mesh=mesh,
        in_specs=(
            P(("row", "col"), None),
            P(("row", "col"), None, None, None),
            P(("row", "col"), None),
            P(),
        ),
        out_specs=P(("row", "col"), None),
        check_vma=False,
    )
```

```python
import functools

import jax
import jax.numpy as jnp
from jax import lax
from jax.experimental import pallas as pl
from jax.experimental.pallas import tpu as pltpu
from jax.sharding import PartitionSpec as P

REACH = 2
MESH = pl.DeviceIdType.MESH
F32 = jnp.float32
BF16 = jnp.bfloat16
CHUNKS = 4
VECTOR_PIECES = 1
PIECES = (4, 3, 1)
VMEM_BYTES = 20 << 20


def dot(a, b):
    return jnp.dot(a, b, preferred_element_type=F32)


def kernel(
    rows_n, cols_n, chunks, vector_pieces, partial_pieces,
    bounds_hbm, columns_hbm, vec_hbm, ham_hbm, out_ref,
    bounds_ref, columns_ref, ham, band, turned, vec, halo, part_halo, part_send, part_own, part_far, first, image,
    load_sem, ham_sem, small_sem, ready_sem, turn_sem,
    vec_send_sem, vec_recv_sem, part_send_sem, part_recv_sem,
):
    here = ham.shape[0]
    slots = ham.shape[1]
    block = ham.shape[2]
    side = REACH * block
    height = here * block
    width = vec.shape[2]
    total_width = chunks * width
    last = height - side
    devices = rows_n * cols_n
    blocks_all = devices * here
    me = lax.axis_index("row") * cols_n + lax.axis_index("col")
    after = lax.rem(me + 1, devices)
    before = lax.rem(me + devices - 1, devices)
    right = (after // cols_n, lax.rem(after, cols_n))
    left = (before // cols_n, lax.rem(before, cols_n))

    row, col = lax.axis_index("row"), lax.axis_index("col")
    run = cols_n // 2
    core = lax.rem(row, 2)
    far = lax.rem(row // 2, 2) * (col // run)
    at_end = (lax.rem(col, run) == run - 1).astype(jnp.int32)
    leads = at_end * (1 - lax.rem(core + far, 2))
    follows = at_end - leads
    partner = (row + 1 - 2 * core, col)

    turn = 1

    barrier = pltpu.get_barrier_semaphore()
    pl.semaphore_signal(barrier, inc=1, device_id=left, device_id_type=MESH)

    @pl.when(follows == 1)
    def _():
        pl.semaphore_signal(barrier, inc=1, device_id=partner, device_id_type=MESH)


    def lanes(c):
        return pl.ds(pl.multiple_of(c * width, width), width)

    def load(c):
        return pltpu.make_async_copy(vec_hbm.at[:, lanes(c)], vec.at[c], load_sem.at[c])

    def send_vectors(kind, k):
        part = pl.ds(k * (total_width // vector_pieces), total_width // vector_pieces)
        return pltpu.make_async_remote_copy(
            src_ref=vec_hbm.at[pl.ds(last * kind, side), part],
            dst_ref=halo.at[kind, :, part],
            send_sem=vec_send_sem.at[kind, k],
            recv_sem=vec_recv_sem.at[kind, k],
            device_id=(left, right)[kind],
            device_id_type=MESH,
        )

    def send_partial(kind, k):
        part = pl.ds(*partial_pieces[k])
        return pltpu.make_async_remote_copy(
            src_ref=part_send.at[kind, :, part],
            dst_ref=part_halo.at[kind, :, part],
            send_sem=part_send_sem.at[kind, k],
            recv_sem=part_recv_sem.at[kind, k],
            device_id=(left, right)[kind],
            device_id_type=MESH,
        )

    pl.semaphore_wait(barrier, 1 + leads)

    for k in range(vector_pieces):
        send_vectors(1, k).start()

    pl.semaphore_signal(ready_sem, inc=1, device_id=right, device_id_type=MESH)

    small = [
        pltpu.make_async_copy(columns_hbm, columns_ref, small_sem.at[0]),
        pltpu.make_async_copy(bounds_hbm, bounds_ref, small_sem.at[1]),
    ]
    for copy in small:
        copy.start()
    ham_copy = pltpu.make_async_copy(ham_hbm, ham, ham_sem)
    ham_copy.start()

    @pl.loop(0, chunks)
    def _(c):
        load(c).start()

    pl.semaphore_wait(ready_sem, 1)

    for k in range(vector_pieces):
        send_vectors(0, k).start()

    for copy in small:
        copy.wait()
    ham_copy.wait()
    band[...] = jnp.zeros_like(band)

    @pl.loop(0, here)
    def _(r):
        held = [ham[r, k].astype(F32) for k in range(slots)]
        for offset in range(2 * REACH + 1):
            place = r + offset
            target = lax.rem(me * here + place - REACH + blocks_all, blocks_all)
            total = None
            for k in range(slots):
                term = held[k] * jnp.where(columns_ref[r, k] == target, 1.0, 0.0)
                total = term if total is None else total + term
            band[
                pl.ds(pl.multiple_of(r * block, block), block),
                pl.ds(pl.multiple_of(place * block, block), block),
            ] = total.astype(BF16)

    turned[0] = band[pl.ds(0, side), pl.ds(0, side)].astype(F32).T.astype(BF16)
    turned[1] = band[pl.ds(last, side), pl.ds(height + side, side)].astype(F32).T.astype(BF16)

    low, high = bounds_ref[0], bounds_ref[1]
    center = jnp.full((1, width), 0.5 * (high + low), F32)
    inverse = 1.0 / jnp.full((1, width), 0.5 * (high - low), F32)
    double = 2.0 * inverse

    top, bottom = pl.ds(0, side), pl.ds(last, side)
    middle = pl.ds(side, height - 2 * side)
    upper, lower = pl.ds(0, height - side), pl.ds(side, height - side)
    all_in = pl.ds(side, height)
    upper_in, lower_in = pl.ds(side, height - side), pl.ds(2 * side, height - side)

    @pl.loop(0, chunks)
    def _(c):
        load(c).wait()
        top_part = (
            dot(band[top, upper_in], vec[c, upper]) - center * vec[c, top].astype(F32)
        ) * inverse
        part_own[0, c] = top_part
        part_send[0, :, lanes(c)] = top_part.astype(BF16)
        bottom_part = (
            dot(band[bottom, lower_in], vec[c, lower]) - center * vec[c, bottom].astype(F32)
        ) * inverse
        part_own[1, c] = bottom_part
        part_send[1, :, lanes(c)] = bottom_part.astype(BF16)

    @pl.loop(0, chunks)
    def _(c):
        part_far[0, :, lanes(c)] = dot(turned[0], vec[c, top]) * inverse
        part_far[1, :, lanes(c)] = dot(turned[1], vec[c, bottom]) * inverse

    for k in range(len(partial_pieces)):
        send_partial(0, k).start()

    @pl.when(follows == 0)
    def _():
        for k in range(len(partial_pieces)):
            send_partial(1, k).start()

    @pl.loop(0, chunks)
    def _(c):
        first[c, middle] = (
            (dot(band[middle, all_in], vec[c]) - center * vec[c, middle].astype(F32)) * inverse
        ).astype(BF16)

    @pl.when(leads == 1)
    def _():
        for k in range(turn):
            send_partial(1, k).wait_send()
        pl.semaphore_signal(turn_sem, inc=1, device_id=partner, device_id_type=MESH)

    @pl.when(follows == 1)
    def _():
        pl.semaphore_wait(turn_sem, 1)
        for k in range(len(partial_pieces)):
            send_partial(1, k).start()

    def second(c):
        first[c, top] = (
            part_own[0, c] + dot(band[top, pl.ds(0, side)], halo[1, :, lanes(c)]) * inverse
        ).astype(BF16)
        first[c, bottom] = (
            part_own[1, c]
            + dot(band[bottom, pl.ds(height + side, side)], halo[0, :, lanes(c)]) * inverse
        ).astype(BF16)
        out_ref[middle, lanes(c)] = (
            (dot(band[middle, all_in], first[c]) - center * first[c, middle].astype(F32)) * double
            - vec[c, middle].astype(F32)
        ).astype(BF16)
        image[0, :, lanes(c)] = (
            dot(band[top, upper_in], first[c, upper]) - center * first[c, top].astype(F32)
        ) * double - vec[c, top].astype(F32)
        image[1, :, lanes(c)] = (
            dot(band[bottom, lower_in], first[c, lower]) - center * first[c, bottom].astype(F32)
        ) * double - vec[c, bottom].astype(F32)

    for k in range(vector_pieces):
        send_vectors(0, k).wait_recv()
        send_vectors(1, k).wait_recv()
        pl.loop(k * chunks // vector_pieces, (k + 1) * chunks // vector_pieces)(second)

    for k, piece in enumerate(partial_pieces):
        part = pl.ds(*piece)
        scale = jnp.broadcast_to(double[:, :1], (1, piece[1]))
        for kind, rows, beside in (
            (0, bottom, pl.ds(height + side, side)),
            (1, top, pl.ds(0, side)),
        ):
            send_partial(kind, k).wait_recv()
            beyond = part_halo[kind, :, part].astype(F32) + part_far[1 - kind, :, part]
            out_ref[rows, part] = (
                image[1 - kind, :, part] + dot(band[rows, beside], beyond.astype(BF16)) * scale
            ).astype(BF16)

    @pl.when(leads == 0)
    def _():
        for k in range(turn):
            send_partial(1, k).wait_send()

    for k in range(turn, len(partial_pieces)):
        send_partial(1, k).wait_send()
    for k in range(len(partial_pieces)):
        send_partial(0, k).wait_send()
    for kind in range(2):
        for k in range(vector_pieces):
            send_vectors(kind, k).wait_send()


def per_device(rows_n, cols_n, vectors, ham_blocks, ham_columns, bounds):
    height, vec_width = vectors.shape
    here, slots, block, _ = ham_blocks.shape
    side = REACH * block
    chunks = CHUNKS
    width = vec_width // chunks
    pieces = []
    for share in PIECES:
        start = sum(size for _, size in pieces)
        pieces.append((start, vec_width * share // sum(PIECES)))
    return pl.pallas_call(
        functools.partial(kernel, rows_n, cols_n, chunks, VECTOR_PIECES, tuple(pieces)),
        out_shape=jax.ShapeDtypeStruct((height, vec_width), BF16),
        in_specs=[
            pl.BlockSpec(memory_space=pltpu.HBM),
            pl.BlockSpec(memory_space=pltpu.HBM),
            pl.BlockSpec(memory_space=pltpu.HBM),
            pl.BlockSpec(memory_space=pltpu.HBM),
        ],
        out_specs=pl.BlockSpec(memory_space=pltpu.VMEM),
        scratch_shapes=[
            pltpu.SMEM(bounds.shape, F32),
            pltpu.SMEM(ham_columns.shape, jnp.int32),
            pltpu.VMEM((here, slots, block, block), BF16),
            pltpu.VMEM((height, height + 2 * side), BF16),
            pltpu.VMEM((2, side, side), BF16),
            pltpu.VMEM((chunks, height, width), BF16),
            pltpu.VMEM((2, side, vec_width), BF16),
            pltpu.VMEM((2, side, vec_width), BF16),
            pltpu.VMEM((2, side, vec_width), BF16),
            pltpu.VMEM((2, chunks, side, width), F32),
            pltpu.VMEM((2, side, vec_width), F32),
            pltpu.VMEM((chunks, height, width), BF16),
            pltpu.VMEM((2, side, vec_width), F32),
            pltpu.SemaphoreType.DMA((chunks,)),
            pltpu.SemaphoreType.DMA,
            pltpu.SemaphoreType.DMA((2,)),
            pltpu.SemaphoreType.REGULAR,
            pltpu.SemaphoreType.REGULAR,
            pltpu.SemaphoreType.DMA((2, VECTOR_PIECES)),
            pltpu.SemaphoreType.DMA((2, VECTOR_PIECES)),
            pltpu.SemaphoreType.DMA((2, len(pieces))),
            pltpu.SemaphoreType.DMA((2, len(pieces))),
        ],
        compiler_params=pltpu.CompilerParams(
            collective_id=0, has_side_effects=True, vmem_limit_bytes=VMEM_BYTES
        ),
    )(*[pltpu.with_memory_space_constraint(a, pltpu.HBM) for a in (bounds, ham_columns, vectors, ham_blocks)])


def solution(mesh):
    return jax.shard_map(
        functools.partial(per_device, mesh.shape["row"], mesh.shape["col"]),
        mesh=mesh,
        in_specs=(
            P(("row", "col"), None),
            P(("row", "col"), None, None, None),
            P(("row", "col"), None),
            P(),
        ),
        out_specs=P(("row", "col"), None),
        check_vma=False,
    )
```
